32 devices in a mesh: tm: 4 (over z), space: 8 (over y, x, core).
Axes of the slice: x: 2, y: 2, z: 4, core: 2. Of those that a mesh axis runs over, the one named last changes fastest.
Arguments:
- wind: float32 [2, 4, 64, 512], P(None, 'tm', 'space'), may hold values from -0.3 to 0.3
- decay: float32 [4, 3, 64, 512], P('tm', None, 'space'), may hold values from 0.5 to 0.98
- inverse_error_variance: float32 [4, 3, 64, 512], P('tm', None, 'space'), may hold values from 0.5 to 2
- obs_index: int32 [4, 32768], P('tm', 'space'), may hold values from 0 to 12287
- obs_weight: float32 [4, 32768], P('tm', 'space'), may hold values from 0.5 to 4
- innovations: float32 [4, 32768], P('tm', 'space'), may hold values from -6 to 6
Outputs:
- increment: float32 [4, 3, 64, 512], P('tm', None, 'space')
- residual: float32 [4, 3, 64, 512], P('tm', None, 'space')
The draws below stay inside these ranges and needn't reach their ends.
Inputs may be any that keep to these rules, and one draw needn't show every extreme that they name: `obs_index`: each observation names a flattened (field, row, column) cell of the tile of the same subwindow and tile that holds the observation; several observations may name one cell.
All inputs are finite; a program needn't handle non-finite values.
Results may differ from the reference program's by a relative error of at most 0.0001.
Values sent between devices are 32-bit elements; how exact they have to be, the bound alone decides.
A program may use at most 64 MiB of HBM per device.

```python
import math
import jax
import jax.numpy as jnp

CX = 8
NY = 512
OBS_DEV = 4096
STEPS = 4
ITERS = 2
SUBW = 4
NX = 64
OBS = 32768
N_SPACE = 8


def place_ends(array, own_key, least, high):
    place = [jax.random.randint(jax.random.fold_in(own_key, axis), (), 0, length) for axis, length in enumerate(array.shape)]
    longest = array.shape.index(max(array.shape))
    neighbour = place[:longest] + [(place[longest] + 1) % array.shape[longest]] + place[longest + 1:]
    return array.at[tuple(place)].set(least).at[tuple(neighbour)].set(high)


def block_levels(stream_key, shape, cuts, smallest, high):
    level = 1.0
    for position, shards_of in cuts:
        steps = jax.random.uniform(jax.random.fold_in(jax.random.fold_in(stream_key, 6), position), (shards_of,), jnp.float32, smallest / len(cuts), high / len(cuts))
        level = level * jnp.repeat(jnp.exp(steps), shape[position] // shards_of).reshape((-1,) + (1,) * (len(shape) - 1 - position))
    return level


def centred(key, extent, deviation, bound, cuts=(), kind=jnp.bfloat16):
    level = block_levels(key, extent, cuts, -0.22, 0.18) if cuts else 1.0
    values = jax.random.normal(key, extent, jnp.float32) * deviation * level
    return jnp.minimum(jnp.maximum(values, -bound), bound).astype(kind)


def setup_inputs(seed: int = 0) -> dict:
    keys = jax.random.split(jax.random.key(seed), 7)
    return {
        "wind": jnp.clip(jax.random.uniform(keys[0], (2, SUBW, NX, NY), jnp.float32, -0.3, 0.3) * block_levels(keys[0], (2, SUBW, NX, NY), ((1, 4), (2, 8)), -0.4, 0.0), -0.3, 0.3),
        "decay": jnp.clip(0.5 + 0.48000002 * jax.random.uniform(keys[1], (SUBW, 3, NX, NY), jnp.float32) ** block_levels(keys[1], (SUBW, 3, NX, NY), ((0, 4), (2, 8)), -0.2, 0.2), 0.5, 0.98),
        "inverse_error_variance": jnp.clip(jnp.exp(math.log(2.0) - 1.3862944 * jax.random.uniform(keys[2], (SUBW, 3, NX, NY), jnp.float32) ** block_levels(keys[2], (SUBW, 3, NX, NY), ((0, 4), (2, 8)), -0.2, 0.2)), 0.5, 2.0),
        "obs_index": place_ends(jax.random.randint(keys[3], (SUBW, OBS), 0, 3 * CX * NY), jax.random.fold_in(keys[3], 1), 0, (3 * CX * NY) - 1).astype(jnp.int32),
        "obs_weight": jnp.clip(jnp.exp(math.log(4.0) - 2.0794415 * jax.random.uniform(keys[4], (SUBW, OBS), jnp.float32) ** block_levels(keys[4], (SUBW, OBS), ((0, 4), (1, 8)), -0.2, 0.2)), 0.5, 4.0),
        "innovations": centred(keys[5], (SUBW, OBS), 1.0, 6.0, ((0, 4), (1, 8)), jnp.float32),
    }


diffusion = 0.15


def along_rows(u):
    zero_row = jnp.zeros_like(u[:, :, :1])
    upper = jnp.concatenate([u[:, :, 1:], zero_row], axis=2)
    lower = jnp.concatenate([zero_row, u[:, :, :-1]], axis=2)
    return upper, lower


def along_cols(u):
    zero_col = jnp.zeros_like(u[..., :1])
    right = jnp.concatenate([u[..., 1:], zero_col], axis=3)
    left = jnp.concatenate([zero_col, u[..., :-1]], axis=3)
    return right, left


def perturbation_propagator(u, eastward_velocity, northward_velocity):
    upper, lower = along_rows(u)
    right, left = along_cols(u)
    laplace = upper + lower + right + left - 4.0 * u
    return u + diffusion * laplace - 0.5 * eastward_velocity * (upper - lower) - 0.5 * northward_velocity * (right - left)


def adjoint_step(v, eastward_velocity, northward_velocity):
    upper, lower = along_rows(v)
    right, left = along_cols(v)
    laplace = upper + lower + right + left - 4.0 * v
    upper_w, lower_w = along_rows(eastward_velocity * v)
    right_z, left_solution = along_cols(northward_velocity * v)
    return v + diffusion * laplace + 0.5 * (upper_w - lower_w) + 0.5 * (right_z - left_solution)


def tiles(field):
    return field.reshape(SUBW, 3, N_SPACE, CX, NY).transpose(0, 2, 1, 3, 4).reshape(SUBW, N_SPACE, 3 * CX * NY)


def untile(tiled):
    return tiled.reshape(SUBW, N_SPACE, 3, CX, NY).transpose(0, 2, 1, 3, 4).reshape(SUBW, 3, NX, NY)


def scatter_obs(values, index):
    def one(vals, idx):
        return jax.ops.segment_sum(vals, idx, num_segments=3 * CX * NY)
    return untile(jax.vmap(jax.vmap(one))(values, index))


def precondition(r, decay):
    v_rows = [None] * SUBW
    v_rows[SUBW - 1] = r[SUBW - 1]
    for k in range(SUBW - 2, -1, -1):
        v_rows[k] = r[k] + decay[k] * v_rows[k + 1]
    u_rows = [v_rows[0]]
    for k in range(1, SUBW):
        u_rows.append(v_rows[k] + decay[k - 1] * u_rows[k - 1])
    return jnp.stack(u_rows)


def reference(wind, decay, inverse_error_variance, obs_index, obs_weight, innovations):
    eastward_velocity = wind[0][:, None]
    northward_velocity = wind[1][:, None]
    index = obs_index.reshape(SUBW, N_SPACE, OBS_DEV)
    weight = obs_weight.reshape(SUBW, N_SPACE, OBS_DEV)
    departures = innovations.reshape(SUBW, N_SPACE, OBS_DEV)

    def hessian(conjugate_update_vector):
        predicted_state_grid = conjugate_update_vector
        for step in range(STEPS):
            predicted_state_grid = perturbation_propagator(predicted_state_grid, eastward_velocity, northward_velocity)
        displaced_grid_values = jnp.concatenate([jnp.zeros_like(predicted_state_grid[:1]), predicted_state_grid[:-1]], axis=0)
        mismatch = inverse_error_variance * (conjugate_update_vector - displaced_grid_values)
        back = jnp.concatenate([mismatch[1:], jnp.zeros_like(mismatch[:1])], axis=0)
        for step in range(STEPS):
            back = adjoint_step(back, eastward_velocity, northward_velocity)
        picked = jnp.take_along_axis(tiles(conjugate_update_vector), index, axis=2)
        return mismatch - back + scatter_obs(weight * picked, index)

    increment = jnp.zeros((SUBW, 3, NX, NY), jnp.float32)
    residual = scatter_obs(weight * departures, index)
    precond = precondition(residual, decay)
    direction = precond
    rz_now = jnp.sum(residual * precond)
    for it in range(ITERS):
        image = hessian(direction)
        alpha = rz_now / jnp.sum(direction * image)
        increment = increment + alpha * direction
        residual = residual - alpha * image
        if it + 1 < ITERS:
            precond = precondition(residual, decay)
            upcoming_residual_dot = jnp.sum(residual * precond)
            direction = precond + (upcoming_residual_dot / rz_now) * direction
            rz_now = upcoming_residual_dot
    return increment, residual
```

```python
import functools

import jax
import jax.numpy as jnp
from jax import lax
from jax.experimental import pallas as pl
from jax.experimental.pallas import tpu as pltpu
from jax.sharding import PartitionSpec as P

STEPS = 4
DIFFUSION = 0.15
MESH = pl.DeviceIdType.MESH
CHUNK = 1024


def split3(x):
    high = x.astype(jnp.bfloat16)
    rest = x - high.astype(jnp.float32)
    mid = rest.astype(jnp.bfloat16)
    low = (rest - mid.astype(jnp.float32)).astype(jnp.bfloat16)
    return high, mid, low


def folded(x):
    rows = x[0] + x[1] + x[2]
    width = rows.shape[1]
    total = rows[:, :128]
    for at in range(128, width, 128):
        total = total + rows[:, at : at + 128]
    return total


def whole(x):
    return jnp.sum(x, axis=(0, 1), keepdims=True)


def kernel(
    n_tm, n_sp, wind, decay, iev, obs, weight, innov, inc_out, res_out,
    dec_all, r_all, q_all, z_all, y_all, wind_ext, iev_next, iev_ext, d_ext, f_send, f_recv,
    sum_tm, sum_sp, diag, tm_send, tm_recv, sp_send, sp_recv, st_send, st_recv,
):
    k = lax.axis_index("tm")
    s = lax.axis_index("space")
    fields, rows, width = decay.shape[1:]
    has_next, has_prev = k < n_tm - 1, k > 0
    has_high, has_low = s < n_sp - 1, s > 0
    pending = []

    def tm_at(o):
        return lax.rem(k + o + n_tm, n_tm)

    def sp_at(o):
        return lax.rem(s + o + n_sp, n_sp)

    barrier = pltpu.get_barrier_semaphore()
    for o in range(1, n_tm):
        pl.semaphore_signal(barrier, inc=1, device_id=(tm_at(o), s), device_id_type=MESH)
    for o in range(1, n_sp):
        pl.semaphore_signal(barrier, inc=1, device_id=(k, sp_at(o)), device_id_type=MESH)
    pl.semaphore_wait(barrier, n_tm + n_sp - 2)

    def remote(src, dst, send, recv, device):
        return pltpu.make_async_remote_copy(
            src_ref=src, dst_ref=dst, send_sem=send, recv_sem=recv,
            device_id=device, device_id_type=MESH,
        )

    def start(copy, cond=None):
        pending.append((copy, cond))
        if cond is None:
            copy.start()
        else:
            pl.when(cond)(copy.start)

    def spread_tm(buffer, use):
        for o in range(1, n_tm):
            start(remote(buffer.at[k], buffer.at[k], tm_send.at[use, o], tm_recv.at[use, o], (tm_at(o), s)))

    def arrive_tm(buffer, use):
        for o in range(1, n_tm):
            src = tm_at(-o)
            remote(buffer.at[src], buffer.at[src], tm_send.at[use, o], tm_recv.at[use, o], (src, s)).wait_recv()

    def spread_sp(buffer, use):
        for o in range(1, n_sp):
            start(remote(buffer.at[s], buffer.at[s], sp_send.at[use, o], sp_recv.at[use, o], (k, sp_at(o))))

    def arrive_sp(buffer, use):
        for o in range(1, n_sp):
            src = sp_at(-o)
            remote(buffer.at[src], buffer.at[src], sp_send.at[use, o], sp_recv.at[use, o], (k, src)).wait_recv()

    def to_sides(src, dst, use, cond=None):
        up = has_high if cond is None else jnp.logical_and(has_high, cond)
        down = has_low if cond is None else jnp.logical_and(has_low, cond)
        start(remote(src, dst.at[0], st_send.at[use], st_recv.at[use], (k, sp_at(1))), up)
        start(remote(src, dst.at[1], st_send.at[use + 1], st_recv.at[use + 1], (k, sp_at(-1))), down)

    def from_sides(src, dst, use, cond=None):
        up = has_low if cond is None else jnp.logical_and(has_low, cond)
        down = has_high if cond is None else jnp.logical_and(has_high, cond)
        pl.when(up)(remote(src, dst.at[0], st_send.at[use], st_recv.at[use], (k, sp_at(-1))).wait_recv)
        pl.when(down)(remote(src, dst.at[1], st_send.at[use + 1], st_recv.at[use + 1], (k, sp_at(1))).wait_recv)

    start(remote(iev.at[0], iev_next, st_send.at[0], st_recv.at[0], (tm_at(-1), s)), has_prev)
    to_sides(wind.at[:, 0], wind_ext, 2)
    dec_all[k] = decay[0]
    spread_tm(dec_all, 0)

    blocks = width // 128
    tiles = fields * blocks * rows
    n_obs = obs.shape[1]
    acc = jnp.zeros((6 * tiles, 128), jnp.float32)
    for at in range(0, n_obs, CHUNK):
        part = pl.ds(at, CHUNK)
        cell = obs[:, part]
        wgt = weight[:, part]
        field = cell // (rows * width)
        row = lax.rem(cell // width, rows)
        block = lax.rem(cell // 128, blocks)
        tile = (field * blocks + block) * rows + row
        lane = jnp.bitwise_and(cell, 127)
        left = (lax.broadcasted_iota(jnp.int32, (tiles, CHUNK), 0) == tile).astype(jnp.float32)
        left = left.astype(jnp.bfloat16).reshape(tiles // 16, 16, CHUNK)
        right = (lax.broadcasted_iota(jnp.int32, (128, CHUNK), 0) == lane).astype(jnp.float32).astype(jnp.bfloat16)
        parts = []
        for values in (wgt, wgt * innov[:, part]):
            for piece in split3(jnp.broadcast_to(values, (16, CHUNK))):
                parts.append((left * piece[None]).reshape(tiles, CHUNK))
        acc = acc + lax.dot_general(
            jnp.concatenate(parts, axis=0), right, (((1,), (1,)), ((), ())),
            preferred_element_type=jnp.float32,
        )

    def total(which):
        base = 3 * which * tiles
        x = acc[base : base + tiles] + acc[base + tiles : base + 2 * tiles] + acc[base + 2 * tiles : base + 3 * tiles]
        return jnp.stack([
            jnp.concatenate([x[(f * blocks + b) * rows :][:rows] for b in range(blocks)], axis=1)
            for f in range(fields)
        ])

    diag[...] = total(0)
    r_all[k] = total(1)
    spread_tm(r_all, 1)

    from_sides(wind.at[:, 0], wind_ext, 2)
    pl.when(has_next)(remote(iev.at[0], iev_next, st_send.at[0], st_recv.at[0], (tm_at(1), s)).wait_recv)
    to_sides(iev_next, iev_ext, 4, has_next)
    zero = jnp.zeros((rows, width), jnp.float32)
    flow = [
        jnp.concatenate([
            jnp.where(has_low, wind_ext[0, c], zero), wind[c, 0], jnp.where(has_high, wind_ext[1, c], zero)
        ], axis=0)
        for c in range(2)
    ]
    line = lax.broadcasted_iota(jnp.int32, (3 * rows, width), 0)
    column = lax.broadcasted_iota(jnp.int32, (3 * rows, width), 1)
    inside = jnp.logical_and(line + (s - 1) * rows >= 0, line + (s - 1) * rows < n_sp * rows)
    mask = inside.astype(jnp.float32)
    own = mask * (1.0 - 4.0 * DIFFUSION)
    c_up = mask * (DIFFUSION - 0.5 * flow[0])
    c_down = mask * (DIFFUSION + 0.5 * flow[0])
    c_right = jnp.where(column < width - 1, mask * (DIFFUSION - 0.5 * flow[1]), 0.0)
    c_left = jnp.where(column > 0, mask * (DIFFUSION + 0.5 * flow[1]), 0.0)
    high = 3 * rows - 1

    def model(u):
        for _ in range(STEPS):
            u = (
                own * u + c_up * pltpu.roll(u, high, 0) + c_down * pltpu.roll(u, 1, 0)
                + c_right * pltpu.roll(u, width - 1, 1) + c_left * pltpu.roll(u, 1, 1)
            )
        return u

    def adjoint(v):
        for _ in range(STEPS):
            v = (
                own * v + pltpu.roll(c_up * v, 1, 0) + pltpu.roll(c_down * v, high, 0)
                + pltpu.roll(c_right * v, 1, 1) + pltpu.roll(c_left * v, width - 1, 1)
            )
        return v

    def precondition(source, target):
        for f in range(fields):
            v = [source[j, f] for j in range(n_tm)]
            for j in range(n_tm - 2, -1, -1):
                v[j] = v[j] + dec_all[j, f] * v[j + 1]
            for j in range(1, n_tm):
                v[j] = v[j] + dec_all[j - 1, f] * v[j - 1]
            for j in range(n_tm):
                target[j, f] = v[j]

    def send_pair(source, it):
        to_sides(source.at[pl.ds(k, 2)], d_ext.at[it], 6 + 2 * it)

    def hessian(source, it, first):
        from_sides(source.at[pl.ds(k, 2)], d_ext.at[it], 6 + 2 * it)

        def three(which, f):
            return jnp.concatenate([
                jnp.where(has_low, d_ext[it, 0, which, f], zero), source[k + which, f],
                jnp.where(has_high, d_ext[it, 1, which, f], zero),
            ], axis=0)

        ahead = []
        for f in range(fields):
            ahead.append(model(three(0, f)))
            f_send[it, f] = ahead[f][rows : 2 * rows]
        start(remote(f_send.at[it], f_recv.at[it], st_send.at[10 + it], st_recv.at[10 + it], (tm_at(1), s)), has_next)
        if first:
            from_sides(iev_next, iev_ext, 4, has_next)
        low_ok, high_ok = jnp.logical_and(has_low, has_next), jnp.logical_and(has_high, has_next)
        backs = []
        for f in range(fields):
            inverse = jnp.concatenate([
                jnp.where(low_ok, iev_ext[0, f], zero), jnp.where(has_next, iev_next[f], zero),
                jnp.where(high_ok, iev_ext[1, f], zero),
            ], axis=0)
            backs.append(adjoint(inverse * (three(1, f) - ahead[f]))[rows : 2 * rows])
        pl.when(has_prev)(
            remote(f_send.at[it], f_recv.at[it], st_send.at[10 + it], st_recv.at[10 + it], (tm_at(-1), s)).wait_recv
        )
        image = []
        for f in range(fields):
            p = source[k, f]
            displaced = jnp.where(has_prev, f_recv[it, f], zero)
            image.append(iev[0, f] * (p - displaced) - backs[f] + diag[f] * p)
        return jnp.stack(image)

    z_all[n_tm] = jnp.zeros_like(z_all[n_tm])
    y_all[n_tm] = jnp.zeros_like(y_all[n_tm])
    arrive_tm(dec_all, 0)
    arrive_tm(r_all, 1)
    precondition(r_all, z_all)
    send_pair(z_all, 0)
    q = hessian(z_all, 0, True)
    z = z_all[k]
    r = r_all[k]
    sum_tm[0, k, 0] = folded(r * z)
    sum_tm[0, k, 1] = folded(z * q)
    q_all[k] = q
    spread_tm(sum_tm.at[0], 3)
    spread_tm(q_all, 2)
    arrive_tm(sum_tm.at[0], 3)
    sum_sp[0, s] = jnp.sum(sum_tm[0], axis=0)
    spread_sp(sum_sp.at[0], 0)
    arrive_tm(q_all, 2)
    precondition(q_all, y_all)
    send_pair(y_all, 1)
    w = hessian(y_all, 1, False)
    arrive_sp(sum_sp.at[0], 0)
    sums = jnp.sum(sum_sp[0], axis=0)
    rz, dq = whole(sums[0]), whole(sums[1])
    alpha = rz / dq
    z = z_all[k]
    r = r_all[k]
    q = q_all[k]
    r2 = r - alpha * q
    z2 = z - alpha * y_all[k]
    az2 = q - alpha * w
    sum_tm[1, k, 0] = folded(r2 * z2)
    sum_tm[1, k, 1] = folded(z2 * az2)
    sum_tm[1, k, 2] = folded(z2 * q + z * az2)
    spread_tm(sum_tm.at[1], 4)
    arrive_tm(sum_tm.at[1], 4)
    sum_sp[1, s] = jnp.sum(sum_tm[1], axis=0)
    spread_sp(sum_sp.at[1], 1)
    arrive_sp(sum_sp.at[1], 1)
    sums = jnp.sum(sum_sp[1], axis=0)
    rz2 = whole(sums[0])
    beta = rz2 / rz
    alpha2 = rz2 / (whole(sums[1]) + beta * whole(sums[2]) + beta * beta * dq)
    inc_out[0] = alpha * z + alpha2 * (z2 + beta * z)
    res_out[0] = r2 - alpha2 * (az2 + beta * q)
    for copy, cond in pending:
        if cond is None:
            copy.wait_send()
        else:
            pl.when(cond)(copy.wait_send)


def on_device(wind, decay, iev, obs, weight, innov):
    n_tm, n_sp = lax.axis_size("tm"), lax.axis_size("space")
    tile = decay.shape[1:]
    f32 = jnp.float32
    vmem = pl.BlockSpec(memory_space=pltpu.VMEM)
    field = jax.ShapeDtypeStruct(decay.shape, f32)
    return pl.pallas_call(
        functools.partial(kernel, n_tm, n_sp),
        out_shape=(field, field),
        in_specs=[vmem] * 6,
        out_specs=(vmem, vmem),
        scratch_shapes=[
            pltpu.VMEM((n_tm,) + tile, f32),
            pltpu.VMEM((n_tm,) + tile, f32),
            pltpu.VMEM((n_tm,) + tile, f32),
            pltpu.VMEM((n_tm + 1,) + tile, f32),
            pltpu.VMEM((n_tm + 1,) + tile, f32),
            pltpu.VMEM((2, 2) + tile[1:], f32),
            pltpu.VMEM(tile, f32),
            pltpu.VMEM((2,) + tile, f32),
            pltpu.VMEM((2, 2, 2) + tile, f32),
            pltpu.VMEM((2,) + tile, f32),
            pltpu.VMEM((2,) + tile, f32),
            pltpu.VMEM((2, n_tm, 3, 8, 128), f32),
            pltpu.VMEM((2, n_sp, 3, 8, 128), f32),
            pltpu.VMEM(tile, f32),
            pltpu.SemaphoreType.DMA((5, n_tm)),
            pltpu.SemaphoreType.DMA((5, n_tm)),
            pltpu.SemaphoreType.DMA((2, n_sp)),
            pltpu.SemaphoreType.DMA((2, n_sp)),
            pltpu.SemaphoreType.DMA((12,)),
            pltpu.SemaphoreType.DMA((12,)),
        ],
        compiler_params=pltpu.CompilerParams(
            collective_id=0, has_side_effects=True, vmem_limit_bytes=48 * 1024 * 1024
        ),
    )(wind, decay, iev, obs, weight, innov)


def solution(mesh):
    placed = (
        P(None, "tm", "space", None),
        P("tm", None, "space", None),
        P("tm", None, "space", None),
        P("tm", "space"),
        P("tm", "space"),
        P("tm", "space"),
    )
    return jax.shard_map(
        on_device,
        mesh=mesh,
        in_specs=placed,
        out_specs=(P("tm", None, "space", None), P("tm", None, "space", None)),
        check_vma=False,
    )
```

```python
import functools

import jax
import jax.numpy as jnp
from jax import lax
from jax.experimental import pallas as pl
from jax.experimental.pallas import tpu as pltpu
from jax.sharding import PartitionSpec as P

STEPS = 4
DIFFUSION = 0.15
MESH = pl.DeviceIdType.MESH
CHUNK = 1024


def split3(x):
    high = x.astype(jnp.bfloat16)
    rest = x - high.astype(jnp.float32)
    mid = rest.astype(jnp.bfloat16)
    low = (rest - mid.astype(jnp.float32)).astype(jnp.bfloat16)
    return high, mid, low


def folded(x):
    total = x[:, :128]
    for at in range(128, x.shape[1], 128):
        total = total + x[:, at : at + 128]
    return total


def packed(*terms):
    line = lax.broadcasted_iota(jnp.int32, (8, 128), 0)
    out = jnp.zeros((8, 128), jnp.float32)
    for at, term in enumerate(terms):
        out = jnp.where(line == at, jnp.sum(term, axis=0, keepdims=True), out)
    return out


def whole(x, at):
    return jnp.sum(x[at : at + 1], axis=1, keepdims=True)


def kernel(
    n_tm, n_sp, wind_in, decay_in, iev_in, obs_in, weight_in, innov_in, out,
    wind, decay, iev, obs, weight, innov, load_sem, dec_all, r_all, q_all, z_all, y_all, wind_ext, wind_prev, wind_prev_ext, iev_next, iev_ext, d_ext, pack,
    sum_tm, sum_sp, diag, tm_send, tm_recv, sp_send, sp_recv, st_send, st_recv,
):
    k = lax.axis_index("tm")
    s = lax.axis_index("space")
    fields, rows, width = decay_in.shape[1:]
    has_next, has_prev = k < n_tm - 1, k > 0
    has_high, has_low = s < n_sp - 1, s > 0
    pending = []

    def tm_at(o):
        return lax.rem(k + o + n_tm, n_tm)

    def sp_at(o):
        return lax.rem(s + o + n_sp, n_sp)

    loads = [
        pltpu.make_async_copy(src, dst, load_sem.at[at])
        for at, (src, dst) in enumerate((
            (obs_in, obs), (weight_in, weight), (innov_in, innov),
            (decay_in, decay), (iev_in, iev), (wind_in, wind),
        ))
    ]
    for load in loads:
        load.start()
    barrier = pltpu.get_barrier_semaphore()
    for o in range(1, n_tm):
        pl.semaphore_signal(barrier, inc=1, device_id=(tm_at(o), s), device_id_type=MESH)
    for o in range(1, n_sp):
        pl.semaphore_signal(barrier, inc=1, device_id=(k, sp_at(o)), device_id_type=MESH)
    pl.semaphore_wait(barrier, n_tm + n_sp - 2)

    def remote(src, dst, send, recv, device):
        return pltpu.make_async_remote_copy(
            src_ref=src, dst_ref=dst, send_sem=send, recv_sem=recv,
            device_id=device, device_id_type=MESH,
        )

    def start(copy, cond=None):
        pending.append((copy, cond))
        if cond is None:
            copy.start()
        else:
            pl.when(cond)(copy.start)

    def spread_tm(pick, use, f=0):
        for o in range(1, n_tm):
            start(remote(pick(k), pick(k), tm_send.at[use, f, o], tm_recv.at[use, f, o], (tm_at(o), s)))

    def arrive_tm(pick, use, f=0):
        for o in range(1, n_tm):
            src = tm_at(-o)
            remote(pick(src), pick(src), tm_send.at[use, f, o], tm_recv.at[use, f, o], (src, s)).wait_recv()

    def spread_sp(buffer, use):
        for o in range(1, n_sp):
            start(remote(buffer.at[s], buffer.at[s], sp_send.at[use, o], sp_recv.at[use, o], (k, sp_at(o))))

    def arrive_sp(buffer, use):
        for o in range(1, n_sp):
            src = sp_at(-o)
            remote(buffer.at[src], buffer.at[src], sp_send.at[use, o], sp_recv.at[use, o], (k, src)).wait_recv()

    def both(first, second):
        return first if second is None else jnp.logical_and(first, second)

    def to_sides(up, down, low, high, use, cond=None):
        start(remote(up, low, st_send.at[use], st_recv.at[use], (k, sp_at(1))), both(has_high, cond))
        start(remote(down, high, st_send.at[use + 1], st_recv.at[use + 1], (k, sp_at(-1))), both(has_low, cond))

    def from_sides(up, down, low, high, use, cond=None):
        pl.when(both(has_low, cond))(
            remote(up, low, st_send.at[use], st_recv.at[use], (k, sp_at(-1))).wait_recv)
        pl.when(both(has_high, cond))(
            remote(down, high, st_send.at[use + 1], st_recv.at[use + 1], (k, sp_at(1))).wait_recv)

    winds = (wind.at[:, 0], wind.at[:, 0], wind_ext.at[0], wind_ext.at[1], 2)
    ievs = (iev_next, iev_next, iev_ext.at[0], iev_ext.at[1], 4, has_next)
    prevs = (wind_prev, wind_prev, wind_prev_ext.at[0], wind_prev_ext.at[1], 6, has_prev)

    for load in loads:
        load.wait()

    start(remote(iev.at[0], iev_next, st_send.at[0], st_recv.at[0], (tm_at(-1), s)), has_prev)
    start(remote(wind.at[:, 0], wind_prev, st_send.at[1], st_recv.at[1], (tm_at(1), s)), has_next)
    to_sides(*winds)
    dec_all[k] = decay[0]
    for f in range(fields):
        spread_tm(lambda j: dec_all.at[j, f], 0, f)

    blocks = width // 128
    tiles = fields * blocks * rows
    n_obs = obs.shape[1]
    acc = jnp.zeros((6 * tiles, 128), jnp.float32)
    for at in range(0, n_obs, CHUNK):
        part = pl.ds(at, CHUNK)
        cell = obs[:, part]
        wgt = weight[:, part]
        field = cell // (rows * width)
        row = lax.rem(cell // width, rows)
        block = lax.rem(cell // 128, blocks)
        tile = (field * blocks + block) * rows + row
        lane = jnp.bitwise_and(cell, 127)
        left = (lax.broadcasted_iota(jnp.int32, (tiles, CHUNK), 0) == tile).astype(jnp.float32)
        left = left.astype(jnp.bfloat16).reshape(tiles // 16, 16, CHUNK)
        right = (lax.broadcasted_iota(jnp.int32, (128, CHUNK), 0) == lane).astype(jnp.float32).astype(jnp.bfloat16)
        parts = []
        for values in (wgt, wgt * innov[:, part]):
            for piece in split3(jnp.broadcast_to(values, (16, CHUNK))):
                parts.append((left * piece[None]).reshape(tiles, CHUNK))
        acc = acc + lax.dot_general(
            jnp.concatenate(parts, axis=0), right, (((1,), (1,)), ((), ())),
            preferred_element_type=jnp.float32,
        )

    def total(which):
        base = 3 * which * tiles
        x = acc[base : base + tiles] + acc[base + tiles : base + 2 * tiles] + acc[base + 2 * tiles : base + 3 * tiles]
        return jnp.stack([
            jnp.concatenate([x[(f * blocks + b) * rows :][:rows] for b in range(blocks)], axis=1)
            for f in range(fields)
        ])

    r_all[k] = total(1)
    for f in range(fields):
        spread_tm(lambda j: r_all.at[j, f], 1, f)
    diag[...] = total(0)

    pl.when(has_next)(remote(iev.at[0], iev_next, st_send.at[0], st_recv.at[0], (tm_at(1), s)).wait_recv)
    to_sides(*ievs)
    pl.when(has_prev)(remote(wind.at[:, 0], wind_prev, st_send.at[1], st_recv.at[1], (tm_at(-1), s)).wait_recv)
    to_sides(*prevs)
    zero = jnp.zeros((rows, width), jnp.float32)
    high = 3 * rows - 1
    half = rows // 2
    top = lax.broadcasted_iota(jnp.int32, (rows, width), 0) < half

    def three(low, mid, upper):
        return jnp.concatenate([jnp.where(has_low, low, zero), mid, jnp.where(has_high, upper, zero)], axis=0)

    def coefficients(flow):
        line = lax.broadcasted_iota(jnp.int32, (3 * rows, width), 0)
        column = lax.broadcasted_iota(jnp.int32, (3 * rows, width), 1)
        inside = jnp.logical_and(line + (s - 1) * rows >= 0, line + (s - 1) * rows < n_sp * rows)
        mask = inside.astype(jnp.float32)
        return (
            mask * (1.0 - 4.0 * DIFFUSION),
            mask * (DIFFUSION - 0.5 * flow[0]),
            mask * (DIFFUSION + 0.5 * flow[0]),
            jnp.where(column < width - 1, mask * (DIFFUSION - 0.5 * flow[1]), 0.0),
            jnp.where(column > 0, mask * (DIFFUSION + 0.5 * flow[1]), 0.0),
        )

    def model(u, by):
        own, c_up, c_down, c_right, c_left = by
        for _ in range(STEPS):
            u = (
                own * u + c_up * pltpu.roll(u, high, 0) + c_down * pltpu.roll(u, 1, 0)
                + c_right * pltpu.roll(u, width - 1, 1) + c_left * pltpu.roll(u, 1, 1)
            )
        return u

    def adjoint(v, by):
        own, c_up, c_down, c_right, c_left = by
        for _ in range(STEPS):
            v = (
                own * v + pltpu.roll(c_up * v, 1, 0) + pltpu.roll(c_down * v, high, 0)
                + pltpu.roll(c_right * v, 1, 1) + pltpu.roll(c_left * v, width - 1, 1)
            )
        return v

    def precondition(source, target, f):
        v = [source[j, f] for j in range(n_tm)]
        for j in range(n_tm - 2, -1, -1):
            v[j] = v[j] + dec_all[j, f] * v[j + 1]
        for j in range(1, n_tm):
            v[j] = v[j] + dec_all[j - 1, f] * v[j - 1]
        for j in range(n_tm):
            target[j + 1, f] = v[j]

    def pairs(it, f):
        return (pack.at[it, 0, f], pack.at[it, 1, f], d_ext.at[it, 0, f], d_ext.at[it, 1, f], 8 + 2 * (fields * it + f))

    def send_pair(source, it, f):
        before, here, after = pltpu.roll(source[k, f], half, 0), source[k + 1, f], source[k + 2, f]
        pack[it, 0, f, 0] = here
        pack[it, 1, f, 0] = here
        pack[it, 0, f, 1] = jnp.where(top, before, after)
        pack[it, 1, f, 1] = jnp.where(top, after, before)
        to_sides(*pairs(it, f))

    def hessian(source, it, f):
        from_sides(*pairs(it, f))
        p = source[k + 1, f]
        low, upper = d_ext[it, 0, f, 1], d_ext[it, 1, f, 1]
        ahead = model(three(d_ext[it, 0, f, 0], p, d_ext[it, 1, f, 0]), by_here)
        inverse = jnp.where(has_next, three(iev_ext[0, f], iev_next[f], iev_ext[1, f]), 0.0)
        back = adjoint(inverse * (three(low, source[k + 2, f], upper) - ahead), by_here)[rows : 2 * rows]
        before = three(pltpu.roll(low, half, 0), source[k, f], pltpu.roll(upper, half, 0))
        displaced = model(before, by_prev)[rows : 2 * rows]
        return iev[0, f] * (p - displaced) - back + diag[f] * p

    for edge in (0, n_tm + 1):
        z_all[edge] = jnp.zeros_like(z_all[edge])
        y_all[edge] = jnp.zeros_like(y_all[edge])
    from_sides(*winds)
    by_here = coefficients([three(wind_ext[0, c], wind[c, 0], wind_ext[1, c]) for c in range(2)])
    for f in range(fields):
        arrive_tm(lambda j: dec_all.at[j, f], 0, f)
        arrive_tm(lambda j: r_all.at[j, f], 1, f)
        precondition(r_all, z_all, f)
        send_pair(z_all, 0, f)
    from_sides(*ievs)
    from_sides(*prevs)
    by_prev = coefficients([
        jnp.where(has_prev, three(wind_prev_ext[0, c], wind_prev[c], wind_prev_ext[1, c]), 0.0) for c in range(2)
    ])
    rz_part = dq_part = 0.0
    for f in range(fields):
        q = hessian(z_all, 0, f)
        q_all[k, f] = q
        spread_tm(lambda j: q_all.at[j, f], 2, f)
        z = z_all[k + 1, f]
        rz_part = rz_part + folded(r_all[k, f] * z)
        dq_part = dq_part + folded(z * q)
    sum_tm[0, k] = packed(rz_part, dq_part)
    spread_tm(lambda j: sum_tm.at[0, j], 3)
    for f in range(fields):
        arrive_tm(lambda j: q_all.at[j, f], 2, f)
        precondition(q_all, y_all, f)
        send_pair(y_all, 1, f)
    arrive_tm(lambda j: sum_tm.at[0, j], 3)
    sum_sp[0, s] = jnp.sum(sum_tm[0], axis=0)
    spread_sp(sum_sp.at[0], 0)
    w = [hessian(y_all, 1, f) for f in range(fields)]
    arrive_sp(sum_sp.at[0], 0)
    sums = jnp.sum(sum_sp[0], axis=0)
    rz, dq = whole(sums, 0), whole(sums, 1)
    alpha = rz / dq
    parts = [0.0, 0.0, 0.0]
    held = []
    for f in range(fields):
        z, q = z_all[k + 1, f], q_all[k, f]
        r2 = r_all[k, f] - alpha * q
        z2 = z - alpha * y_all[k + 1, f]
        az2 = q - alpha * w[f]
        parts[0] = parts[0] + folded(r2 * z2)
        parts[1] = parts[1] + folded(z2 * az2)
        parts[2] = parts[2] + folded(z2 * q + z * az2)
        held.append((r2, z2, az2))
    sum_tm[1, k] = packed(*parts)
    spread_tm(lambda j: sum_tm.at[1, j], 4)
    arrive_tm(lambda j: sum_tm.at[1, j], 4)
    sum_sp[1, s] = jnp.sum(sum_tm[1], axis=0)
    spread_sp(sum_sp.at[1], 1)
    arrive_sp(sum_sp.at[1], 1)
    sums = jnp.sum(sum_sp[1], axis=0)
    rz2 = whole(sums, 0)
    beta = rz2 / rz
    alpha2 = rz2 / (whole(sums, 1) + beta * whole(sums, 2) + beta * beta * dq)
    for f in range(fields):
        r2, z2, az2 = held[f]
        z, q = z_all[k + 1, f], q_all[k, f]
        out[0, 0, f] = alpha * z + alpha2 * (z2 + beta * z)
        out[1, 0, f] = r2 - alpha2 * (az2 + beta * q)
    for copy, cond in pending:
        if cond is None:
            copy.wait_send()
        else:
            pl.when(cond)(copy.wait_send)


def on_device(wind, decay, iev, obs, weight, innov):
    n_tm, n_sp = lax.axis_size("tm"), lax.axis_size("space")
    tile = decay.shape[1:]
    f32 = jnp.float32
    vmem = pl.BlockSpec(memory_space=pltpu.VMEM)
    both = pl.pallas_call(
        functools.partial(kernel, n_tm, n_sp),
        out_shape=jax.ShapeDtypeStruct((2,) + decay.shape, f32),
        in_specs=[pl.BlockSpec(memory_space=pltpu.HBM)] * 6,
        out_specs=vmem,
        scratch_shapes=[
            pltpu.VMEM(wind.shape, f32),
            pltpu.VMEM(decay.shape, f32),
            pltpu.VMEM(iev.shape, f32),
            pltpu.VMEM(obs.shape, jnp.int32),
            pltpu.VMEM(weight.shape, f32),
            pltpu.VMEM(innov.shape, f32),
            pltpu.SemaphoreType.DMA((6,)),
            pltpu.VMEM((n_tm,) + tile, f32),
            pltpu.VMEM((n_tm,) + tile, f32),
            pltpu.VMEM((n_tm,) + tile, f32),
            pltpu.VMEM((n_tm + 2,) + tile, f32),
            pltpu.VMEM((n_tm + 2,) + tile, f32),
            pltpu.VMEM((2, 2) + tile[1:], f32),
            pltpu.VMEM((2,) + tile[1:], f32),
            pltpu.VMEM((2, 2) + tile[1:], f32),
            pltpu.VMEM(tile, f32),
            pltpu.VMEM((2,) + tile, f32),
            pltpu.VMEM((2, 2, tile[0], 2) + tile[1:], f32),
            pltpu.VMEM((2, 2, tile[0], 2) + tile[1:], f32),
            pltpu.VMEM((2, n_tm, 8, 128), f32),
            pltpu.VMEM((2, n_sp, 8, 128), f32),
            pltpu.VMEM(tile, f32),
            pltpu.SemaphoreType.DMA((5, 3, n_tm)),
            pltpu.SemaphoreType.DMA((5, 3, n_tm)),
            pltpu.SemaphoreType.DMA((2, n_sp)),
            pltpu.SemaphoreType.DMA((2, n_sp)),
            pltpu.SemaphoreType.DMA((20,)),
            pltpu.SemaphoreType.DMA((20,)),
        ],
        compiler_params=pltpu.CompilerParams(
            collective_id=0, has_side_effects=True, vmem_limit_bytes=62 * 1024 * 1024
        ),
    )(wind, decay, iev, obs, weight, innov)
    return both[0], both[1]


def solution(mesh):
    placed = (
        P(None, "tm", "space", None),
        P("tm", None, "space", None),
        P("tm", None, "space", None),
        P("tm", "space"),
        P("tm", "space"),
        P("tm", "space"),
    )
    return jax.shard_map(
        on_device,
        mesh=mesh,
        in_specs=placed,
        out_specs=(P("tm", None, "space", None), P("tm", None, "space", None)),
        check_vma=False,
    )
```

```python
import functools

import jax
import jax.numpy as jnp
from jax import lax
from jax.experimental import pallas as pl
from jax.experimental.pallas import tpu as pltpu
from jax.sharding import PartitionSpec as P

STEPS = 4
DIFFUSION = 0.15
MESH = pl.DeviceIdType.MESH
CHUNK = 1024
DIRECT = 64


def split3(x):
    high = x.astype(jnp.bfloat16)
    rest = x - high.astype(jnp.float32)
    mid = rest.astype(jnp.bfloat16)
    low = (rest - mid.astype(jnp.float32)).astype(jnp.bfloat16)
    return high, mid, low


def folded(x):
    total = x[:, :128]
    for at in range(128, x.shape[1], 128):
        total = total + x[:, at : at + 128]
    return total


def packed(*terms):
    line = lax.broadcasted_iota(jnp.int32, (8, 128), 0)
    out = jnp.zeros((8, 128), jnp.float32)
    for at, term in enumerate(terms):
        out = jnp.where(line == at, jnp.sum(term, axis=0, keepdims=True), out)
    return out


def whole(x, at):
    return jnp.sum(x[at : at + 1], axis=1, keepdims=True)


def kernel(
    n_tm, n_sp, wind_in, decay_in, iev_in, obs_in, weight_in, innov_in, out,
    wind, decay, iev, obs, weight, innov, load_sem, dec_all, r_all, q_all, z_all, y_all, wind_ext, wind_prev, wind_prev_ext, iev_next, iev_ext, d_ext, pack,
    sum_tm, sum_sp, sum_any, any_send, any_recv, diag, tm_send, tm_recv, sp_send, sp_recv, st_send, st_recv,
):
    k = lax.axis_index("tm")
    s = lax.axis_index("space")
    fields, rows, width = decay_in.shape[1:]
    has_next, has_prev = k < n_tm - 1, k > 0
    has_high, has_low = s < n_sp - 1, s > 0
    pending = []

    def tm_at(o):
        return lax.rem(k + o + n_tm, n_tm)

    def sp_at(o):
        return lax.rem(s + o + n_sp, n_sp)

    loads = [
        pltpu.make_async_copy(src, dst, load_sem.at[at])
        for at, (src, dst) in enumerate((
            (obs_in, obs), (weight_in, weight), (innov_in, innov),
            (decay_in, decay), (iev_in, iev), (wind_in, wind),
        ))
    ]
    for load in loads:
        load.start()
    barrier = pltpu.get_barrier_semaphore()
    me = k * n_sp + s
    direct = n_tm * n_sp <= DIRECT

    def any_at(o):
        return lax.rem(me + o + n_tm * n_sp, n_tm * n_sp)

    def place(at):
        return (at // n_sp, lax.rem(at, n_sp))

    if direct:
        partners = [place(any_at(o)) for o in range(1, n_tm * n_sp)]
    else:
        partners = [(tm_at(o), s) for o in range(1, n_tm)] + [(k, sp_at(o)) for o in range(1, n_sp)]
    for partner in partners:
        pl.semaphore_signal(barrier, inc=1, device_id=partner, device_id_type=MESH)
    pl.semaphore_wait(barrier, len(partners))

    def remote(src, dst, send, recv, device):
        return pltpu.make_async_remote_copy(
            src_ref=src, dst_ref=dst, send_sem=send, recv_sem=recv,
            device_id=device, device_id_type=MESH,
        )

    def start(copy, cond=None):
        pending.append((copy, cond))
        if cond is None:
            copy.start()
        else:
            pl.when(cond)(copy.start)

    def spread_tm(pick, use, f=0):
        for o in range(1, n_tm):
            start(remote(pick(k), pick(k), tm_send.at[use, f, o], tm_recv.at[use, f, o], (tm_at(o), s)))

    def arrive_tm(pick, use, f=0):
        for o in range(1, n_tm):
            src = tm_at(-o)
            remote(pick(src), pick(src), tm_send.at[use, f, o], tm_recv.at[use, f, o], (src, s)).wait_recv()

    def spread_sp(buffer, use):
        for o in range(1, n_sp):
            start(remote(buffer.at[s], buffer.at[s], sp_send.at[use, o], sp_recv.at[use, o], (k, sp_at(o))))

    def arrive_sp(buffer, use):
        for o in range(1, n_sp):
            src = sp_at(-o)
            remote(buffer.at[src], buffer.at[src], sp_send.at[use, o], sp_recv.at[use, o], (k, src)).wait_recv()

    def both(first, second):
        return first if second is None else jnp.logical_and(first, second)

    def to_sides(up, down, low, high, use, cond=None):
        start(remote(up, low, st_send.at[use], st_recv.at[use], (k, sp_at(1))), both(has_high, cond))
        start(remote(down, high, st_send.at[use + 1], st_recv.at[use + 1], (k, sp_at(-1))), both(has_low, cond))

    def from_sides(up, down, low, high, use, cond=None):
        pl.when(both(has_low, cond))(
            remote(up, low, st_send.at[use], st_recv.at[use], (k, sp_at(-1))).wait_recv)
        pl.when(both(has_high, cond))(
            remote(down, high, st_send.at[use + 1], st_recv.at[use + 1], (k, sp_at(1))).wait_recv)

    winds = (wind.at[:, 0], wind.at[:, 0], wind_ext.at[0], wind_ext.at[1], 2)
    ievs = (iev_next, iev_next, iev_ext.at[0], iev_ext.at[1], 4, has_next)
    prevs = (wind_prev, wind_prev, wind_prev_ext.at[0], wind_prev_ext.at[1], 6, has_prev)

    for load in loads:
        load.wait()

    start(remote(iev.at[0], iev_next, st_send.at[0], st_recv.at[0], (tm_at(-1), s)), has_prev)
    start(remote(wind.at[:, 0], wind_prev, st_send.at[1], st_recv.at[1], (tm_at(1), s)), has_next)
    to_sides(*winds)
    dec_all[k] = decay[0]
    for f in range(2):
        spread_tm(lambda j: dec_all.at[j, f], 0, f)

    blocks = width // 128
    tiles = fields * blocks * rows
    n_obs = obs.shape[1]
    acc = jnp.zeros((6 * tiles, 128), jnp.float32)
    for at in range(0, n_obs, CHUNK):
        part = pl.ds(at, CHUNK)
        cell = obs[:, part]
        wgt = weight[:, part]
        field = cell // (rows * width)
        row = lax.rem(cell // width, rows)
        block = lax.rem(cell // 128, blocks)
        tile = (field * blocks + block) * rows + row
        lane = jnp.bitwise_and(cell, 127)
        left = (lax.broadcasted_iota(jnp.int32, (tiles, CHUNK), 0) == tile).astype(jnp.float32)
        left = left.astype(jnp.bfloat16).reshape(tiles // 16, 16, CHUNK)
        right = (lax.broadcasted_iota(jnp.int32, (128, CHUNK), 0) == lane).astype(jnp.float32).astype(jnp.bfloat16)
        parts = []
        for values in (wgt, wgt * innov[:, part]):
            for piece in split3(jnp.broadcast_to(values, (16, CHUNK))):
                parts.append((left * piece[None]).reshape(tiles, CHUNK))
        acc = acc + lax.dot_general(
            jnp.concatenate(parts, axis=0), right, (((1,), (1,)), ((), ())),
            preferred_element_type=jnp.float32,
        )

    def total(which):
        base = 3 * which * tiles
        x = acc[base : base + tiles] + acc[base + tiles : base + 2 * tiles] + acc[base + 2 * tiles : base + 3 * tiles]
        return jnp.stack([
            jnp.concatenate([x[(f * blocks + b) * rows :][:rows] for b in range(blocks)], axis=1)
            for f in range(fields)
        ])

    r_all[k] = total(1)
    for f in range(fields):
        spread_tm(lambda j: r_all.at[j, f], 1, f)
        if f + 2 < fields:
            spread_tm(lambda j: dec_all.at[j, f + 2], 0, f + 2)
    diag[...] = total(0)

    pl.when(has_next)(remote(iev.at[0], iev_next, st_send.at[0], st_recv.at[0], (tm_at(1), s)).wait_recv)
    to_sides(*ievs)
    pl.when(has_prev)(remote(wind.at[:, 0], wind_prev, st_send.at[1], st_recv.at[1], (tm_at(-1), s)).wait_recv)
    to_sides(*prevs)
    zero = jnp.zeros((rows, width), jnp.float32)
    high = 3 * rows - 1
    half = rows // 2
    top = lax.broadcasted_iota(jnp.int32, (rows, width), 0) < half

    def three(low, mid, upper):
        return jnp.concatenate([jnp.where(has_low, low, zero), mid, jnp.where(has_high, upper, zero)], axis=0)

    def coefficients(flow):
        line = lax.broadcasted_iota(jnp.int32, (3 * rows, width), 0)
        column = lax.broadcasted_iota(jnp.int32, (3 * rows, width), 1)
        inside = jnp.logical_and(line + (s - 1) * rows >= 0, line + (s - 1) * rows < n_sp * rows)
        mask = inside.astype(jnp.float32)
        return (
            mask * (1.0 - 4.0 * DIFFUSION),
            mask * (DIFFUSION - 0.5 * flow[0]),
            mask * (DIFFUSION + 0.5 * flow[0]),
            jnp.where(column < width - 1, mask * (DIFFUSION - 0.5 * flow[1]), 0.0),
            jnp.where(column > 0, mask * (DIFFUSION + 0.5 * flow[1]), 0.0),
        )

    def model(u, by):
        own, c_up, c_down, c_right, c_left = by
        for _ in range(STEPS):
            u = (
                own * u + c_up * pltpu.roll(u, high, 0) + c_down * pltpu.roll(u, 1, 0)
                + c_right * pltpu.roll(u, width - 1, 1) + c_left * pltpu.roll(u, 1, 1)
            )
        return u

    def adjoint(v, by):
        own, c_up, c_down, c_right, c_left = by
        for _ in range(STEPS):
            v = (
                own * v + pltpu.roll(c_up * v, 1, 0) + pltpu.roll(c_down * v, high, 0)
                + pltpu.roll(c_right * v, 1, 1) + pltpu.roll(c_left * v, width - 1, 1)
            )
        return v

    def precondition(source, target, f):
        v = [source[j, f] for j in range(n_tm)]
        for j in range(n_tm - 2, -1, -1):
            v[j] = v[j] + dec_all[j, f] * v[j + 1]
        for j in range(1, n_tm):
            v[j] = v[j] + dec_all[j - 1, f] * v[j - 1]
        for j in range(n_tm):
            target[j + 1, f] = v[j]

    def pairs(it, f):
        return (pack.at[it, 0, f], pack.at[it, 1, f], d_ext.at[it, 0, f], d_ext.at[it, 1, f], 8 + 2 * (fields * it + f))

    def send_pair(source, it, f):
        before, here, after = pltpu.roll(source[k, f], half, 0), source[k + 1, f], source[k + 2, f]
        pack[it, 0, f, 0] = here
        pack[it, 1, f, 0] = here
        pack[it, 0, f, 1] = jnp.where(top, before, after)
        pack[it, 1, f, 1] = jnp.where(top, after, before)
        to_sides(*pairs(it, f))

    def hessian(source, it, f):
        from_sides(*pairs(it, f))
        p = source[k + 1, f]
        low, upper = d_ext[it, 0, f, 1], d_ext[it, 1, f, 1]
        before = three(pltpu.roll(low, half, 0), source[k, f], pltpu.roll(upper, half, 0))
        jump = p - model(before, by_prev)[rows : 2 * rows]

        def close():
            ahead = model(three(d_ext[it, 0, f, 0], p, d_ext[it, 1, f, 0]), by_here)
            inverse = jnp.where(has_next, three(iev_ext[0, f], iev_next[f], iev_ext[1, f]), 0.0)
            back = adjoint(inverse * (three(low, source[k + 2, f], upper) - ahead), by_here)[rows : 2 * rows]
            return iev[0, f] * jump - back + diag[f] * p

        return jump, close

    for edge in (0, n_tm + 1):
        z_all[edge] = jnp.zeros_like(z_all[edge])
        y_all[edge] = jnp.zeros_like(y_all[edge])
    from_sides(*winds)
    by_here = coefficients([three(wind_ext[0, c], wind[c, 0], wind_ext[1, c]) for c in range(2)])
    for f in range(fields):
        arrive_tm(lambda j: dec_all.at[j, f], 0, f)
        arrive_tm(lambda j: r_all.at[j, f], 1, f)
        precondition(r_all, z_all, f)
        send_pair(z_all, 0, f)
    from_sides(*ievs)
    from_sides(*prevs)
    by_prev = coefficients([
        jnp.where(has_prev, three(wind_prev_ext[0, c], wind_prev[c], wind_prev_ext[1, c]), 0.0) for c in range(2)
    ])
    jumps = []
    rz_part = dq_part = 0.0
    for f in range(fields):
        jump, close = hessian(z_all, 0, f)
        jumps.append(jump)
        q = close()
        q_all[k, f] = q
        spread_tm(lambda j: q_all.at[j, f], 2, f)
        z = z_all[k + 1, f]
        rz_part = rz_part + folded(r_all[k, f] * z)
        dq_part = dq_part + folded(z * q)
    sum_tm[0, k] = packed(rz_part, dq_part)
    spread_tm(lambda j: sum_tm.at[0, j], 3)
    for f in range(fields):
        arrive_tm(lambda j: q_all.at[j, f], 2, f)
        precondition(q_all, y_all, f)
        send_pair(y_all, 1, f)
    arrive_tm(lambda j: sum_tm.at[0, j], 3)
    sum_sp[0, s] = jnp.sum(sum_tm[0], axis=0)
    spread_sp(sum_sp.at[0], 0)
    opened = [hessian(y_all, 1, f) for f in range(fields)]
    closes = [close for _, close in opened]
    arrive_sp(sum_sp.at[0], 0)
    sums = jnp.sum(sum_sp[0], axis=0)
    rz, dq = whole(sums, 0), whole(sums, 1)
    alpha = rz / dq
    parts = [0.0, 0.0, 0.0]
    held = []
    for f in range(fields):
        z, q = z_all[k + 1, f], q_all[k, f]
        r2 = r_all[k, f] - alpha * q
        z2 = z - alpha * y_all[k + 1, f]
        jump2 = jumps[f] - alpha * opened[f][0]
        scaled, seen = iev[0, f] * jump2, diag[f] * z2
        parts[0] = parts[0] + folded(r2 * z2)
        parts[1] = parts[1] + folded(scaled * jump2 + seen * z2)
        parts[2] = parts[2] + folded(2.0 * (scaled * jumps[f] + seen * z))
        held.append((r2, z2))
    if direct:
        sum_any[me] = packed(*parts)
        for o in range(1, n_tm * n_sp):
            start(remote(sum_any.at[me], sum_any.at[me], any_send.at[o], any_recv.at[o], place(any_at(o))))
    else:
        sum_tm[1, k] = packed(*parts)
        spread_tm(lambda j: sum_tm.at[1, j], 4)
    w = [close() for close in closes]
    if direct:
        for o in range(1, n_tm * n_sp):
            src = any_at(-o)
            remote(sum_any.at[src], sum_any.at[src], any_send.at[o], any_recv.at[o], place(src)).wait_recv()
        sums = jnp.sum(sum_any[...], axis=0)
    else:
        arrive_tm(lambda j: sum_tm.at[1, j], 4)
        sum_sp[1, s] = jnp.sum(sum_tm[1], axis=0)
        spread_sp(sum_sp.at[1], 1)
        arrive_sp(sum_sp.at[1], 1)
        sums = jnp.sum(sum_sp[1], axis=0)
    rz2 = whole(sums, 0)
    beta = rz2 / rz
    alpha2 = rz2 / (whole(sums, 1) + beta * whole(sums, 2) + beta * beta * dq)
    for f in range(fields):
        r2, z2 = held[f]
        z, q = z_all[k + 1, f], q_all[k, f]
        az2 = q - alpha * w[f]
        out[0, 0, f] = alpha * z + alpha2 * (z2 + beta * z)
        out[1, 0, f] = r2 - alpha2 * (az2 + beta * q)
    for copy, cond in pending:
        if cond is None:
            copy.wait_send()
        else:
            pl.when(cond)(copy.wait_send)


def on_device(wind, decay, iev, obs, weight, innov):
    n_tm, n_sp = lax.axis_size("tm"), lax.axis_size("space")
    tile = decay.shape[1:]
    f32 = jnp.float32
    vmem = pl.BlockSpec(memory_space=pltpu.VMEM)
    both = pl.pallas_call(
        functools.partial(kernel, n_tm, n_sp),
        out_shape=jax.ShapeDtypeStruct((2,) + decay.shape, f32),
        in_specs=[pl.BlockSpec(memory_space=pltpu.HBM)] * 6,
        out_specs=vmem,
        scratch_shapes=[
            pltpu.VMEM(wind.shape, f32),
            pltpu.VMEM(decay.shape, f32),
            pltpu.VMEM(iev.shape, f32),
            pltpu.VMEM(obs.shape, jnp.int32),
            pltpu.VMEM(weight.shape, f32),
            pltpu.VMEM(innov.shape, f32),
            pltpu.SemaphoreType.DMA((6,)),
            pltpu.VMEM((n_tm,) + tile, f32),
            pltpu.VMEM((n_tm,) + tile, f32),
            pltpu.VMEM((n_tm,) + tile, f32),
            pltpu.VMEM((n_tm + 2,) + tile, f32),
            pltpu.VMEM((n_tm + 2,) + tile, f32),
            pltpu.VMEM((2, 2) + tile[1:], f32),
            pltpu.VMEM((2,) + tile[1:], f32),
            pltpu.VMEM((2, 2) + tile[1:], f32),
            pltpu.VMEM(tile, f32),
            pltpu.VMEM((2,) + tile, f32),
            pltpu.VMEM((2, 2, tile[0], 2) + tile[1:], f32),
            pltpu.VMEM((2, 2, tile[0], 2) + tile[1:], f32),
            pltpu.VMEM((2, n_tm, 8, 128), f32),
            pltpu.VMEM((2, n_sp, 8, 128), f32),
            pltpu.VMEM((n_tm * n_sp, 8, 128), f32),
            pltpu.SemaphoreType.DMA((n_tm * n_sp,)),
            pltpu.SemaphoreType.DMA((n_tm * n_sp,)),
            pltpu.VMEM(tile, f32),
            pltpu.SemaphoreType.DMA((5, 3, n_tm)),
            pltpu.SemaphoreType.DMA((5, 3, n_tm)),
            pltpu.SemaphoreType.DMA((2, n_sp)),
            pltpu.SemaphoreType.DMA((2, n_sp)),
            pltpu.SemaphoreType.DMA((20,)),
            pltpu.SemaphoreType.DMA((20,)),
        ],
        compiler_params=pltpu.CompilerParams(
            collective_id=0, has_side_effects=True, vmem_limit_bytes=62 * 1024 * 1024
        ),
    )(wind, decay, iev, obs, weight, innov)
    return both[0], both[1]


def solution(mesh):
    placed = (
        P(None, "tm", "space", None),
        P("tm", None, "space", None),
        P("tm", None, "space", None),
        P("tm", "space"),
        P("tm", "space"),
        P("tm", "space"),
    )
    return jax.shard_map(
        on_device,
        mesh=mesh,
        in_specs=placed,
        out_specs=(P("tm", None, "space", None), P("tm", None, "space", None)),
        check_vma=False,
    )
```

```python
import functools

import jax
import jax.numpy as jnp
from jax import lax
from jax.experimental import pallas as pl
from jax.experimental.pallas import tpu as pltpu
from jax.sharding import PartitionSpec as P

STEPS = 4
DIFFUSION = 0.15
MESH = pl.DeviceIdType.MESH
CHUNK = 1024
DIRECT = 64


def split3(x):
    high = x.astype(jnp.bfloat16)
    rest = x - high.astype(jnp.float32)
    mid = rest.astype(jnp.bfloat16)
    low = (rest - mid.astype(jnp.float32)).astype(jnp.bfloat16)
    return high, mid, low


def folded(x):
    total = x[:, :128]
    for at in range(128, x.shape[1], 128):
        total = total + x[:, at : at + 128]
    return total


def packed(*terms):
    line = lax.broadcasted_iota(jnp.int32, (8, 128), 0)
    out = jnp.zeros((8, 128), jnp.float32)
    for at, term in enumerate(terms):
        out = jnp.where(line == at, jnp.sum(term, axis=0, keepdims=True), out)
    return out


def whole(x, at):
    return jnp.sum(x[at : at + 1], axis=1, keepdims=True)


def kernel(
    n_tm, n_sp, wind_in, decay_in, iev_in, obs_in, weight_in, innov_in, out,
    wind, decay, iev, obs, weight, innov, load_sem, dec_all, r_all, q_all, z_all, y_all, wind_ext, wind_prev, wind_prev_ext, iev_next, iev_ext, d_ext, pack,
    sum_tm, sum_sp, sum_any, any_send, any_recv, diag, tm_send, tm_recv, sp_send, sp_recv, st_send, st_recv,
):
    k = lax.axis_index("tm")
    s = lax.axis_index("space")
    fields, rows, width = decay_in.shape[1:]
    has_next, has_prev = k < n_tm - 1, k > 0
    has_high, has_low = s < n_sp - 1, s > 0
    pending = []

    def tm_at(o):
        return lax.rem(k + o + n_tm, n_tm)

    def sp_at(o):
        return lax.rem(s + o + n_sp, n_sp)

    loads = [
        pltpu.make_async_copy(src, dst, load_sem.at[at])
        for at, (src, dst) in enumerate((
            (decay_in, decay), (iev_in, iev), (wind_in, wind),
            (obs_in, obs), (weight_in, weight), (innov_in, innov),
        ))
    ]
    for load in loads:
        load.start()
    barrier = pltpu.get_barrier_semaphore()
    me = k * n_sp + s
    direct = n_tm * n_sp <= DIRECT

    def any_at(o):
        return lax.rem(me + o + n_tm * n_sp, n_tm * n_sp)

    def place(at):
        return (at // n_sp, lax.rem(at, n_sp))

    if direct:
        partners = [place(any_at(o)) for o in range(1, n_tm * n_sp)]
    else:
        partners = [(tm_at(o), s) for o in range(1, n_tm)] + [(k, sp_at(o)) for o in range(1, n_sp)]
    for partner in partners:
        pl.semaphore_signal(barrier, inc=1, device_id=partner, device_id_type=MESH)
    pl.semaphore_wait(barrier, len(partners))

    def remote(src, dst, send, recv, device):
        return pltpu.make_async_remote_copy(
            src_ref=src, dst_ref=dst, send_sem=send, recv_sem=recv,
            device_id=device, device_id_type=MESH,
        )

    def start(copy, cond=None):
        pending.append((copy, cond))
        if cond is None:
            copy.start()
        else:
            pl.when(cond)(copy.start)

    def spread_tm(pick, use, f=0, cond=None):
        for o in range(1, n_tm):
            start(remote(pick(k), pick(k), tm_send.at[use, f, o], tm_recv.at[use, f, o], (tm_at(o), s)), cond)

    def arrive_tm(pick, use, f=0, count=None):
        for o in range(1, n_tm):
            src = tm_at(-o)
            wait = remote(pick(src), pick(src), tm_send.at[use, f, o], tm_recv.at[use, f, o], (src, s)).wait_recv
            if count is None:
                wait()
            else:
                pl.when(src < count)(wait)

    def spread_sp(buffer, use):
        for o in range(1, n_sp):
            start(remote(buffer.at[s], buffer.at[s], sp_send.at[use, o], sp_recv.at[use, o], (k, sp_at(o))))

    def arrive_sp(buffer, use):
        for o in range(1, n_sp):
            src = sp_at(-o)
            remote(buffer.at[src], buffer.at[src], sp_send.at[use, o], sp_recv.at[use, o], (k, src)).wait_recv()

    def both(first, second):
        return first if second is None else jnp.logical_and(first, second)

    def to_sides(up, down, low, high, use, cond=None):
        start(remote(up, low, st_send.at[use], st_recv.at[use], (k, sp_at(1))), both(has_high, cond))
        start(remote(down, high, st_send.at[use + 1], st_recv.at[use + 1], (k, sp_at(-1))), both(has_low, cond))

    def from_sides(up, down, low, high, use, cond=None):
        pl.when(both(has_low, cond))(
            remote(up, low, st_send.at[use], st_recv.at[use], (k, sp_at(-1))).wait_recv)
        pl.when(both(has_high, cond))(
            remote(down, high, st_send.at[use + 1], st_recv.at[use + 1], (k, sp_at(1))).wait_recv)

    winds = (wind.at[:, 0], wind.at[:, 0], wind_ext.at[0], wind_ext.at[1], 2)
    ievs = (iev_next, iev_next, iev_ext.at[0], iev_ext.at[1], 4, has_next)
    prevs = (wind_prev, wind_prev, wind_prev_ext.at[0], wind_prev_ext.at[1], 6, has_prev)

    loads[0].wait()
    dec_all[k] = decay[0]
    spread_tm(lambda j: dec_all.at[j, 0], 0, 0, has_next)
    for load in loads[1:]:
        load.wait()
    start(remote(iev.at[0], iev_next, st_send.at[0], st_recv.at[0], (tm_at(-1), s)), has_prev)
    start(remote(wind.at[:, 0], wind_prev, st_send.at[1], st_recv.at[1], (tm_at(1), s)), has_next)
    spread_tm(lambda j: dec_all.at[j, 1], 0, 1, has_next)
    to_sides(*winds)

    blocks = width // 128
    tiles = fields * blocks * rows
    n_obs = obs.shape[1]
    acc = jnp.zeros((6 * tiles, 128), jnp.float32)
    for at in range(0, n_obs, CHUNK):
        part = pl.ds(at, CHUNK)
        cell = obs[:, part]
        wgt = weight[:, part]
        field = cell // (rows * width)
        row = lax.rem(cell // width, rows)
        block = lax.rem(cell // 128, blocks)
        tile = (field * blocks + block) * rows + row
        lane = jnp.bitwise_and(cell, 127)
        left = (lax.broadcasted_iota(jnp.int32, (tiles, CHUNK), 0) == tile).astype(jnp.float32)
        left = left.astype(jnp.bfloat16).reshape(tiles // 16, 16, CHUNK)
        right = (lax.broadcasted_iota(jnp.int32, (128, CHUNK), 0) == lane).astype(jnp.float32).astype(jnp.bfloat16)
        parts = []
        for values in (wgt, wgt * innov[:, part]):
            for piece in split3(jnp.broadcast_to(values, (16, CHUNK))):
                parts.append((left * piece[None]).reshape(tiles, CHUNK))
        acc = acc + lax.dot_general(
            jnp.concatenate(parts, axis=0), right, (((1,), (1,)), ((), ())),
            preferred_element_type=jnp.float32,
        )

    def total(which):
        base = 3 * which * tiles
        x = acc[base : base + tiles] + acc[base + tiles : base + 2 * tiles] + acc[base + 2 * tiles : base + 3 * tiles]
        return jnp.stack([
            jnp.concatenate([x[(f * blocks + b) * rows :][:rows] for b in range(blocks)], axis=1)
            for f in range(fields)
        ])

    r_all[k] = total(1)
    for f in range(fields):
        spread_tm(lambda j: r_all.at[j, f], 1, f)
        if f + 2 < fields:
            spread_tm(lambda j: dec_all.at[j, f + 2], 0, f + 2, has_next)
    diag[...] = total(0)

    pl.when(has_next)(remote(iev.at[0], iev_next, st_send.at[0], st_recv.at[0], (tm_at(1), s)).wait_recv)
    to_sides(*ievs)
    pl.when(has_prev)(remote(wind.at[:, 0], wind_prev, st_send.at[1], st_recv.at[1], (tm_at(-1), s)).wait_recv)
    to_sides(*prevs)
    zero = jnp.zeros((rows, width), jnp.float32)
    high = 3 * rows - 1
    half = rows // 2
    top = lax.broadcasted_iota(jnp.int32, (rows, width), 0) < half

    def three(low, mid, upper):
        return jnp.concatenate([jnp.where(has_low, low, zero), mid, jnp.where(has_high, upper, zero)], axis=0)

    def coefficients(flow):
        line = lax.broadcasted_iota(jnp.int32, (3 * rows, width), 0)
        column = lax.broadcasted_iota(jnp.int32, (3 * rows, width), 1)
        inside = jnp.logical_and(line + (s - 1) * rows >= 0, line + (s - 1) * rows < n_sp * rows)
        mask = inside.astype(jnp.float32)
        return (
            mask * (1.0 - 4.0 * DIFFUSION),
            mask * (DIFFUSION - 0.5 * flow[0]),
            mask * (DIFFUSION + 0.5 * flow[0]),
            jnp.where(column < width - 1, mask * (DIFFUSION - 0.5 * flow[1]), 0.0),
            jnp.where(column > 0, mask * (DIFFUSION + 0.5 * flow[1]), 0.0),
        )

    def model(u, by):
        own, c_up, c_down, c_right, c_left = by
        for _ in range(STEPS):
            u = (
                own * u + c_up * pltpu.roll(u, high, 0) + c_down * pltpu.roll(u, 1, 0)
                + c_right * pltpu.roll(u, width - 1, 1) + c_left * pltpu.roll(u, 1, 1)
            )
        return u

    def adjoint(v, by):
        own, c_up, c_down, c_right, c_left = by
        for _ in range(STEPS):
            v = (
                own * v + pltpu.roll(c_up * v, 1, 0) + pltpu.roll(c_down * v, high, 0)
                + pltpu.roll(c_right * v, 1, 1) + pltpu.roll(c_left * v, width - 1, 1)
            )
        return v

    def precondition(source, target, f):
        v = [source[j, f] for j in range(n_tm)]
        for j in range(n_tm - 2, -1, -1):
            v[j] = v[j] + dec_all[j, f] * v[j + 1]
        for j in range(1, n_tm):
            v[j] = v[j] + dec_all[j - 1, f] * v[j - 1]
        for j in range(n_tm):
            target[j + 1, f] = v[j]

    def pairs(it, f):
        return (pack.at[it, 0, f], pack.at[it, 1, f], d_ext.at[it, 0, f], d_ext.at[it, 1, f], 8 + 2 * (fields * it + f))

    def send_pair(source, it, f):
        before, here, after = pltpu.roll(source[k, f], half, 0), source[k + 1, f], source[k + 2, f]
        pack[it, 0, f, 0] = here
        pack[it, 1, f, 0] = here
        pack[it, 0, f, 1] = jnp.where(top, before, after)
        pack[it, 1, f, 1] = jnp.where(top, after, before)
        to_sides(*pairs(it, f))

    def hessian(source, it, f):
        from_sides(*pairs(it, f))
        p = source[k + 1, f]
        low, upper = d_ext[it, 0, f, 1], d_ext[it, 1, f, 1]
        before = three(pltpu.roll(low, half, 0), source[k, f], pltpu.roll(upper, half, 0))
        jump = p - model(before, by_prev)[rows : 2 * rows]

        def close():
            ahead = model(three(d_ext[it, 0, f, 0], p, d_ext[it, 1, f, 0]), by_here)
            inverse = jnp.where(has_next, three(iev_ext[0, f], iev_next[f], iev_ext[1, f]), 0.0)
            back = adjoint(inverse * (three(low, source[k + 2, f], upper) - ahead), by_here)[rows : 2 * rows]
            return iev[0, f] * jump - back + diag[f] * p

        return jump, close

    for edge in (0, n_tm + 1):
        z_all[edge] = jnp.zeros_like(z_all[edge])
        y_all[edge] = jnp.zeros_like(y_all[edge])
    from_sides(*winds)
    by_here = coefficients([three(wind_ext[0, c], wind[c, 0], wind_ext[1, c]) for c in range(2)])
    for f in range(fields):
        arrive_tm(lambda j: dec_all.at[j, f], 0, f, n_tm - 1)
        arrive_tm(lambda j: r_all.at[j, f], 1, f)
        precondition(r_all, z_all, f)
        send_pair(z_all, 0, f)
    from_sides(*ievs)
    from_sides(*prevs)
    by_prev = coefficients([
        jnp.where(has_prev, three(wind_prev_ext[0, c], wind_prev[c], wind_prev_ext[1, c]), 0.0) for c in range(2)
    ])
    jumps = []
    rz_part = dq_part = 0.0
    for f in range(fields):
        jump, close = hessian(z_all, 0, f)
        jumps.append(jump)
        q = close()
        q_all[k, f] = q
        spread_tm(lambda j: q_all.at[j, f], 2, f)
        z = z_all[k + 1, f]
        rz_part = rz_part + folded(r_all[k, f] * z)
        dq_part = dq_part + folded(z * q)
    sum_tm[0, k] = packed(rz_part, dq_part)
    spread_tm(lambda j: sum_tm.at[0, j], 3)
    for f in range(fields):
        arrive_tm(lambda j: q_all.at[j, f], 2, f)
        precondition(q_all, y_all, f)
        send_pair(y_all, 1, f)
    arrive_tm(lambda j: sum_tm.at[0, j], 3)
    sum_sp[0, s] = jnp.sum(sum_tm[0], axis=0)
    spread_sp(sum_sp.at[0], 0)
    opened = [hessian(y_all, 1, f) for f in range(fields)]
    closes = [close for _, close in opened]
    arrive_sp(sum_sp.at[0], 0)
    sums = jnp.sum(sum_sp[0], axis=0)
    rz, dq = whole(sums, 0), whole(sums, 1)
    alpha = rz / dq
    parts = [0.0, 0.0, 0.0]
    held = []
    for f in range(fields):
        z, q = z_all[k + 1, f], q_all[k, f]
        r2 = r_all[k, f] - alpha * q
        z2 = z - alpha * y_all[k + 1, f]
        jump2 = jumps[f] - alpha * opened[f][0]
        scaled, seen = iev[0, f] * jump2, diag[f] * z2
        parts[0] = parts[0] + folded(r2 * z2)
        parts[1] = parts[1] + folded(scaled * jump2 + seen * z2)
        parts[2] = parts[2] + folded(2.0 * (scaled * jumps[f] + seen * z))
        held.append((r2, z2))
    if direct:
        sum_any[me] = packed(*parts)
        for o in range(1, n_tm * n_sp):
            start(remote(sum_any.at[me], sum_any.at[me], any_send.at[o], any_recv.at[o], place(any_at(o))))
    else:
        sum_tm[1, k] = packed(*parts)
        spread_tm(lambda j: sum_tm.at[1, j], 4)
    w = [close() for close in closes]
    if direct:
        for o in range(1, n_tm * n_sp):
            src = any_at(-o)
            remote(sum_any.at[src], sum_any.at[src], any_send.at[o], any_recv.at[o], place(src)).wait_recv()
        sums = jnp.sum(sum_any[...], axis=0)
    else:
        arrive_tm(lambda j: sum_tm.at[1, j], 4)
        sum_sp[1, s] = jnp.sum(sum_tm[1], axis=0)
        spread_sp(sum_sp.at[1], 1)
        arrive_sp(sum_sp.at[1], 1)
        sums = jnp.sum(sum_sp[1], axis=0)
    rz2 = whole(sums, 0)
    beta = rz2 / rz
    alpha2 = rz2 / (whole(sums, 1) + beta * whole(sums, 2) + beta * beta * dq)
    for f in range(fields):
        r2, z2 = held[f]
        z, q = z_all[k + 1, f], q_all[k, f]
        az2 = q - alpha * w[f]
        out[0, 0, f] = alpha * z + alpha2 * (z2 + beta * z)
        out[1, 0, f] = r2 - alpha2 * (az2 + beta * q)
    for copy, cond in pending:
        if cond is None:
            copy.wait_send()
        else:
            pl.when(cond)(copy.wait_send)


def on_device(wind, decay, iev, obs, weight, innov):
    n_tm, n_sp = lax.axis_size("tm"), lax.axis_size("space")
    tile = decay.shape[1:]
    f32 = jnp.float32
    vmem = pl.BlockSpec(memory_space=pltpu.VMEM)
    both = pl.pallas_call(
        functools.partial(kernel, n_tm, n_sp),
        out_shape=jax.ShapeDtypeStruct((2,) + decay.shape, f32),
        in_specs=[pl.BlockSpec(memory_space=pltpu.HBM)] * 6,
        out_specs=vmem,
        scratch_shapes=[
            pltpu.VMEM(wind.shape, f32),
            pltpu.VMEM(decay.shape, f32),
            pltpu.VMEM(iev.shape, f32),
            pltpu.VMEM(obs.shape, jnp.int32),
            pltpu.VMEM(weight.shape, f32),
            pltpu.VMEM(innov.shape, f32),
            pltpu.SemaphoreType.DMA((6,)),
            pltpu.VMEM((n_tm,) + tile, f32),
            pltpu.VMEM((n_tm,) + tile, f32),
            pltpu.VMEM((n_tm,) + tile, f32),
            pltpu.VMEM((n_tm + 2,) + tile, f32),
            pltpu.VMEM((n_tm + 2,) + tile, f32),
            pltpu.VMEM((2, 2) + tile[1:], f32),
            pltpu.VMEM((2,) + tile[1:], f32),
            pltpu.VMEM((2, 2) + tile[1:], f32),
            pltpu.VMEM(tile, f32),
            pltpu.VMEM((2,) + tile, f32),
            pltpu.VMEM((2, 2, tile[0], 2) + tile[1:], f32),
            pltpu.VMEM((2, 2, tile[0], 2) + tile[1:], f32),
            pltpu.VMEM((2, n_tm, 8, 128), f32),
            pltpu.VMEM((2, n_sp, 8, 128), f32),
            pltpu.VMEM((n_tm * n_sp, 8, 128), f32),
            pltpu.SemaphoreType.DMA((n_tm * n_sp,)),
            pltpu.SemaphoreType.DMA((n_tm * n_sp,)),
            pltpu.VMEM(tile, f32),
            pltpu.SemaphoreType.DMA((5, 3, n_tm)),
            pltpu.SemaphoreType.DMA((5, 3, n_tm)),
            pltpu.SemaphoreType.DMA((2, n_sp)),
            pltpu.SemaphoreType.DMA((2, n_sp)),
            pltpu.SemaphoreType.DMA((20,)),
            pltpu.SemaphoreType.DMA((20,)),
        ],
        compiler_params=pltpu.CompilerParams(
            collective_id=0, has_side_effects=True, vmem_limit_bytes=62 * 1024 * 1024
        ),
    )(wind, decay, iev, obs, weight, innov)
    return both[0], both[1]


def solution(mesh):
    placed = (
        P(None, "tm", "space", None),
        P("tm", None, "space", None),
        P("tm", None, "space", None),
        P("tm", "space"),
        P("tm", "space"),
        P("tm", "space"),
    )
    return jax.shard_map(
        on_device,
        mesh=mesh,
        in_specs=placed,
        out_specs=(P("tm", None, "space", None), P("tm", None, "space", None)),
        check_vma=False,
    )
```

```python
import functools

import jax
import jax.numpy as jnp
from jax import lax
from jax.experimental import pallas as pl
from jax.experimental.pallas import tpu as pltpu
from jax.sharding import PartitionSpec as P

STEPS = 4
DIFFUSION = 0.15
MESH = pl.DeviceIdType.MESH
CHUNK = 1024
DIRECT = 64


def split3(x):
    high = x.astype(jnp.bfloat16)
    rest = x - high.astype(jnp.float32)
    mid = rest.astype(jnp.bfloat16)
    low = (rest - mid.astype(jnp.float32)).astype(jnp.bfloat16)
    return high, mid, low


def folded(x):
    total = x[:, :128]
    for at in range(128, x.shape[1], 128):
        total = total + x[:, at : at + 128]
    return total


def packed(*terms):
    line = lax.broadcasted_iota(jnp.int32, (8, 128), 0)
    out = jnp.zeros((8, 128), jnp.float32)
    for at, term in enumerate(terms):
        out = jnp.where(line == at, jnp.sum(term, axis=0, keepdims=True), out)
    return out


def whole(x, at):
    return jnp.sum(x[at : at + 1], axis=1, keepdims=True)


def kernel(
    n_tm, n_sp, wind_in, decay_in, iev_in, obs_in, weight_in, innov_in, out,
    wind, decay, iev, obs, weight, innov, load_sem, dec_all, r_all, q_all, z_all, y_all, wind_ext, wind_prev, wind_prev_ext, iev_next, iev_ext, d_ext, pack,
    sum_tm, sum_sp, sum_any, any_send, any_recv, diag, tm_send, tm_recv, sp_send, sp_recv, st_send, st_recv,
):
    k = lax.axis_index("tm")
    s = lax.axis_index("space")
    fields, rows, width = decay_in.shape[1:]
    has_next, has_prev = k < n_tm - 1, k > 0
    has_high, has_low = s < n_sp - 1, s > 0
    pending = []

    def tm_at(o):
        return lax.rem(k + o + n_tm, n_tm)

    def sp_at(o):
        return lax.rem(s + o + n_sp, n_sp)

    loads = [
        pltpu.make_async_copy(src, dst, load_sem.at[at])
        for at, (src, dst) in enumerate((
            (decay_in, decay), (iev_in, iev), (wind_in, wind),
            (obs_in, obs), (weight_in, weight), (innov_in, innov),
        ))
    ]
    for load in loads:
        load.start()
    barrier = pltpu.get_barrier_semaphore()
    me = k * n_sp + s
    direct = n_tm * n_sp <= DIRECT

    def any_at(o):
        return lax.rem(me + o + n_tm * n_sp, n_tm * n_sp)

    def place(at):
        return (at // n_sp, lax.rem(at, n_sp))

    if direct:
        partners = [place(any_at(o)) for o in range(1, n_tm * n_sp)]
    else:
        partners = [(tm_at(o), s) for o in range(1, n_tm)] + [(k, sp_at(o)) for o in range(1, n_sp)]
    for partner in partners:
        pl.semaphore_signal(barrier, inc=1, device_id=partner, device_id_type=MESH)
    pl.semaphore_wait(barrier, len(partners))

    def remote(src, dst, send, recv, device):
        return pltpu.make_async_remote_copy(
            src_ref=src, dst_ref=dst, send_sem=send, recv_sem=recv,
            device_id=device, device_id_type=MESH,
        )

    def start(copy, cond=None):
        pending.append((copy, cond))
        if cond is None:
            copy.start()
        else:
            pl.when(cond)(copy.start)

    def spread_tm(pick, use, f=0, cond=None):
        for o in range(1, n_tm):
            start(remote(pick(k), pick(k), tm_send.at[use, f, o], tm_recv.at[use, f, o], (tm_at(o), s)), cond)

    def arrive_tm(pick, use, f=0, count=None):
        for o in range(1, n_tm):
            src = tm_at(-o)
            wait = remote(pick(src), pick(src), tm_send.at[use, f, o], tm_recv.at[use, f, o], (src, s)).wait_recv
            if count is None:
                wait()
            else:
                pl.when(src < count)(wait)

    def spread_sp(buffer, use):
        for o in range(1, n_sp):
            start(remote(buffer.at[s], buffer.at[s], sp_send.at[use, o], sp_recv.at[use, o], (k, sp_at(o))))

    def arrive_sp(buffer, use):
        for o in range(1, n_sp):
            src = sp_at(-o)
            remote(buffer.at[src], buffer.at[src], sp_send.at[use, o], sp_recv.at[use, o], (k, src)).wait_recv()

    def both(first, second):
        return first if second is None else jnp.logical_and(first, second)

    def to_sides(up, down, low, high, use, cond=None):
        start(remote(up, low, st_send.at[use], st_recv.at[use], (k, sp_at(1))), both(has_high, cond))
        start(remote(down, high, st_send.at[use + 1], st_recv.at[use + 1], (k, sp_at(-1))), both(has_low, cond))

    def from_sides(up, down, low, high, use, cond=None):
        pl.when(both(has_low, cond))(
            remote(up, low, st_send.at[use], st_recv.at[use], (k, sp_at(-1))).wait_recv)
        pl.when(both(has_high, cond))(
            remote(down, high, st_send.at[use + 1], st_recv.at[use + 1], (k, sp_at(1))).wait_recv)

    winds = (wind.at[:, 0], wind.at[:, 0], wind_ext.at[0], wind_ext.at[1], 2)
    ievs = (iev_next, iev_next, iev_ext.at[0], iev_ext.at[1], 4, has_next)
    prevs = (wind_prev, wind_prev, wind_prev_ext.at[0], wind_prev_ext.at[1], 6, has_prev)

    loads[0].wait()
    dec_all[k] = decay[0]
    spread_tm(lambda j: dec_all.at[j, 0], 0, 0, has_next)
    spread_tm(lambda j: dec_all.at[j, 1], 0, 1, has_next)
    for load in loads[1:]:
        load.wait()
    start(remote(iev.at[0], iev_next, st_send.at[0], st_recv.at[0], (tm_at(-1), s)), has_prev)
    start(remote(wind.at[:, 0], wind_prev, st_send.at[1], st_recv.at[1], (tm_at(1), s)), has_next)
    to_sides(*winds)

    blocks = width // 128
    tiles = fields * blocks * rows
    n_obs = obs.shape[1]
    acc = jnp.zeros((6 * tiles, 128), jnp.float32)
    for at in range(0, n_obs, CHUNK):
        part = pl.ds(at, CHUNK)
        cell = obs[:, part]
        wgt = weight[:, part]
        field = cell // (rows * width)
        row = lax.rem(cell // width, rows)
        block = lax.rem(cell // 128, blocks)
        tile = (field * blocks + block) * rows + row
        lane = jnp.bitwise_and(cell, 127)
        left = (lax.broadcasted_iota(jnp.int32, (tiles, CHUNK), 0) == tile).astype(jnp.float32)
        left = left.astype(jnp.bfloat16).reshape(tiles // 16, 16, CHUNK)
        right = (lax.broadcasted_iota(jnp.int32, (128, CHUNK), 0) == lane).astype(jnp.float32).astype(jnp.bfloat16)
        parts = []
        for values in (wgt, wgt * innov[:, part]):
            for piece in split3(jnp.broadcast_to(values, (16, CHUNK))):
                parts.append((left * piece[None]).reshape(tiles, CHUNK))
        acc = acc + lax.dot_general(
            jnp.concatenate(parts, axis=0), right, (((1,), (1,)), ((), ())),
            preferred_element_type=jnp.float32,
        )

    def total(which):
        base = 3 * which * tiles
        x = acc[base : base + tiles] + acc[base + tiles : base + 2 * tiles] + acc[base + 2 * tiles : base + 3 * tiles]
        return jnp.stack([
            jnp.concatenate([x[(f * blocks + b) * rows :][:rows] for b in range(blocks)], axis=1)
            for f in range(fields)
        ])

    r_all[k] = total(1)
    for f in range(fields):
        spread_tm(lambda j: r_all.at[j, f], 1, f)
        if f + 2 < fields:
            spread_tm(lambda j: dec_all.at[j, f + 2], 0, f + 2, has_next)
    diag[...] = total(0)

    pl.when(has_next)(remote(iev.at[0], iev_next, st_send.at[0], st_recv.at[0], (tm_at(1), s)).wait_recv)
    to_sides(*ievs)
    pl.when(has_prev)(remote(wind.at[:, 0], wind_prev, st_send.at[1], st_recv.at[1], (tm_at(-1), s)).wait_recv)
    to_sides(*prevs)
    zero = jnp.zeros((rows, width), jnp.float32)
    high = 3 * rows - 1
    half = rows // 2
    top = lax.broadcasted_iota(jnp.int32, (rows, width), 0) < half

    def three(low, mid, upper):
        return jnp.concatenate([jnp.where(has_low, low, zero), mid, jnp.where(has_high, upper, zero)], axis=0)

    def coefficients(flow):
        line = lax.broadcasted_iota(jnp.int32, (3 * rows, width), 0)
        column = lax.broadcasted_iota(jnp.int32, (3 * rows, width), 1)
        inside = jnp.logical_and(line + (s - 1) * rows >= 0, line + (s - 1) * rows < n_sp * rows)
        mask = inside.astype(jnp.float32)
        return (
            mask * (1.0 - 4.0 * DIFFUSION),
            mask * (DIFFUSION - 0.5 * flow[0]),
            mask * (DIFFUSION + 0.5 * flow[0]),
            jnp.where(column < width - 1, mask * (DIFFUSION - 0.5 * flow[1]), 0.0),
            jnp.where(column > 0, mask * (DIFFUSION + 0.5 * flow[1]), 0.0),
        )

    def model(u, by):
        own, c_up, c_down, c_right, c_left = by
        for _ in range(STEPS):
            u = (
                own * u + c_up * pltpu.roll(u, high, 0) + c_down * pltpu.roll(u, 1, 0)
                + c_right * pltpu.roll(u, width - 1, 1) + c_left * pltpu.roll(u, 1, 1)
            )
        return u

    def adjoint(v, by):
        own, c_up, c_down, c_right, c_left = by
        for _ in range(STEPS):
            v = (
                own * v + pltpu.roll(c_up * v, 1, 0) + pltpu.roll(c_down * v, high, 0)
                + pltpu.roll(c_right * v, 1, 1) + pltpu.roll(c_left * v, width - 1, 1)
            )
        return v

    def precondition(source, target, f):
        v = [source[j, f] for j in range(n_tm)]
        for j in range(n_tm - 2, -1, -1):
            v[j] = v[j] + dec_all[j, f] * v[j + 1]
        for j in range(1, n_tm):
            v[j] = v[j] + dec_all[j - 1, f] * v[j - 1]
        for j in range(n_tm):
            target[j + 1, f] = v[j]

    def pairs(it, f):
        return (pack.at[it, 0, f], pack.at[it, 1, f], d_ext.at[it, 0, f], d_ext.at[it, 1, f], 8 + 2 * (fields * it + f))

    def send_pair(source, it, f):
        before, here, after = pltpu.roll(source[k, f], half, 0), source[k + 1, f], source[k + 2, f]
        pack[it, 0, f, 0] = here
        pack[it, 1, f, 0] = here
        pack[it, 0, f, 1] = jnp.where(top, before, after)
        pack[it, 1, f, 1] = jnp.where(top, after, before)
        to_sides(*pairs(it, f))

    def hessian(source, it, f):
        from_sides(*pairs(it, f))
        p = source[k + 1, f]
        low, upper = d_ext[it, 0, f, 1], d_ext[it, 1, f, 1]
        before = three(pltpu.roll(low, half, 0), source[k, f], pltpu.roll(upper, half, 0))
        jump = p - model(before, by_prev)[rows : 2 * rows]

        def close():
            ahead = model(three(d_ext[it, 0, f, 0], p, d_ext[it, 1, f, 0]), by_here)
            inverse = jnp.where(has_next, three(iev_ext[0, f], iev_next[f], iev_ext[1, f]), 0.0)
            back = adjoint(inverse * (three(low, source[k + 2, f], upper) - ahead), by_here)[rows : 2 * rows]
            return iev[0, f] * jump - back + diag[f] * p

        return jump, close

    for edge in (0, n_tm + 1):
        z_all[edge] = jnp.zeros_like(z_all[edge])
        y_all[edge] = jnp.zeros_like(y_all[edge])
    from_sides(*winds)
    by_here = coefficients([three(wind_ext[0, c], wind[c, 0], wind_ext[1, c]) for c in range(2)])
    for f in range(fields):
        arrive_tm(lambda j: dec_all.at[j, f], 0, f, n_tm - 1)
        arrive_tm(lambda j: r_all.at[j, f], 1, f)
        precondition(r_all, z_all, f)
        send_pair(z_all, 0, f)
    from_sides(*ievs)
    from_sides(*prevs)
    by_prev = coefficients([
        jnp.where(has_prev, three(wind_prev_ext[0, c], wind_prev[c], wind_prev_ext[1, c]), 0.0) for c in range(2)
    ])
    jumps = []
    rz_part = dq_part = 0.0
    for f in range(fields):
        jump, close = hessian(z_all, 0, f)
        jumps.append(jump)
        q = close()
        q_all[k, f] = q
        spread_tm(lambda j: q_all.at[j, f], 2, f)
        z = z_all[k + 1, f]
        rz_part = rz_part + folded(r_all[k, f] * z)
        dq_part = dq_part + folded(z * q)
    sum_tm[0, k] = packed(rz_part, dq_part)
    spread_tm(lambda j: sum_tm.at[0, j], 3)
    for f in range(fields):
        arrive_tm(lambda j: q_all.at[j, f], 2, f)
        precondition(q_all, y_all, f)
        send_pair(y_all, 1, f)
    arrive_tm(lambda j: sum_tm.at[0, j], 3)
    sum_sp[0, s] = jnp.sum(sum_tm[0], axis=0)
    spread_sp(sum_sp.at[0], 0)
    opened = [hessian(y_all, 1, f) for f in range(fields)]
    closes = [close for _, close in opened]
    arrive_sp(sum_sp.at[0], 0)
    sums = jnp.sum(sum_sp[0], axis=0)
    rz, dq = whole(sums, 0), whole(sums, 1)
    alpha = rz / dq
    parts = [0.0, 0.0, 0.0]
    held = []
    for f in range(fields):
        z, q = z_all[k + 1, f], q_all[k, f]
        r2 = r_all[k, f] - alpha * q
        z2 = z - alpha * y_all[k + 1, f]
        jump2 = jumps[f] - alpha * opened[f][0]
        scaled, seen = iev[0, f] * jump2, diag[f] * z2
        parts[0] = parts[0] + folded(r2 * z2)
        parts[1] = parts[1] + folded(scaled * jump2 + seen * z2)
        parts[2] = parts[2] + folded(2.0 * (scaled * jumps[f] + seen * z))
        held.append((r2, z2))
    if direct:
        sum_any[me] = packed(*parts)
        for o in range(1, n_tm * n_sp):
            start(remote(sum_any.at[me], sum_any.at[me], any_send.at[o], any_recv.at[o], place(any_at(o))))
    else:
        sum_tm[1, k] = packed(*parts)
        spread_tm(lambda j: sum_tm.at[1, j], 4)
    w = [close() for close in closes]
    if direct:
        for o in range(1, n_tm * n_sp):
            src = any_at(-o)
            remote(sum_any.at[src], sum_any.at[src], any_send.at[o], any_recv.at[o], place(src)).wait_recv()
        sums = jnp.sum(sum_any[...], axis=0)
    else:
        arrive_tm(lambda j: sum_tm.at[1, j], 4)
        sum_sp[1, s] = jnp.sum(sum_tm[1], axis=0)
        spread_sp(sum_sp.at[1], 1)
        arrive_sp(sum_sp.at[1], 1)
        sums = jnp.sum(sum_sp[1], axis=0)
    rz2 = whole(sums, 0)
    beta = rz2 / rz
    alpha2 = rz2 / (whole(sums, 1) + beta * whole(sums, 2) + beta * beta * dq)
    for f in range(fields):
        r2, z2 = held[f]
        z, q = z_all[k + 1, f], q_all[k, f]
        az2 = q - alpha * w[f]
        out[0, 0, f] = alpha * z + alpha2 * (z2 + beta * z)
        out[1, 0, f] = r2 - alpha2 * (az2 + beta * q)
    for copy, cond in pending:
        if cond is None:
            copy.wait_send()
        else:
            pl.when(cond)(copy.wait_send)


def on_device(wind, decay, iev, obs, weight, innov):
    n_tm, n_sp = lax.axis_size("tm"), lax.axis_size("space")
    tile = decay.shape[1:]
    f32 = jnp.float32
    vmem = pl.BlockSpec(memory_space=pltpu.VMEM)
    both = pl.pallas_call(
        functools.partial(kernel, n_tm, n_sp),
        out_shape=jax.ShapeDtypeStruct((2,) + decay.shape, f32),
        in_specs=[pl.BlockSpec(memory_space=pltpu.HBM)] * 6,
        out_specs=vmem,
        scratch_shapes=[
            pltpu.VMEM(wind.shape, f32),
            pltpu.VMEM(decay.shape, f32),
            pltpu.VMEM(iev.shape, f32),
            pltpu.VMEM(obs.shape, jnp.int32),
            pltpu.VMEM(weight.shape, f32),
            pltpu.VMEM(innov.shape, f32),
            pltpu.SemaphoreType.DMA((6,)),
            pltpu.VMEM((n_tm,) + tile, f32),
            pltpu.VMEM((n_tm,) + tile, f32),
            pltpu.VMEM((n_tm,) + tile, f32),
            pltpu.VMEM((n_tm + 2,) + tile, f32),
            pltpu.VMEM((n_tm + 2,) + tile, f32),
            pltpu.VMEM((2, 2) + tile[1:], f32),
            pltpu.VMEM((2,) + tile[1:], f32),
            pltpu.VMEM((2, 2) + tile[1:], f32),
            pltpu.VMEM(tile, f32),
            pltpu.VMEM((2,) + tile, f32),
            pltpu.VMEM((2, 2, tile[0], 2) + tile[1:], f32),
            pltpu.VMEM((2, 2, tile[0], 2) + tile[1:], f32),
            pltpu.VMEM((2, n_tm, 8, 128), f32),
            pltpu.VMEM((2, n_sp, 8, 128), f32),
            pltpu.VMEM((n_tm * n_sp, 8, 128), f32),
            pltpu.SemaphoreType.DMA((n_tm * n_sp,)),
            pltpu.SemaphoreType.DMA((n_tm * n_sp,)),
            pltpu.VMEM(tile, f32),
            pltpu.SemaphoreType.DMA((5, 3, n_tm)),
            pltpu.SemaphoreType.DMA((5, 3, n_tm)),
            pltpu.SemaphoreType.DMA((2, n_sp)),
            pltpu.SemaphoreType.DMA((2, n_sp)),
            pltpu.SemaphoreType.DMA((20,)),
            pltpu.SemaphoreType.DMA((20,)),
        ],
        compiler_params=pltpu.CompilerParams(
            collective_id=0, has_side_effects=True, vmem_limit_bytes=62 * 1024 * 1024
        ),
    )(wind, decay, iev, obs, weight, innov)
    return both[0], both[1]


def solution(mesh):
    placed = (
        P(None, "tm", "space", None),
        P("tm", None, "space", None),
        P("tm", None, "space", None),
        P("tm", "space"),
        P("tm", "space"),
        P("tm", "space"),
    )
    return jax.shard_map(
        on_device,
        mesh=mesh,
        in_specs=placed,
        out_specs=(P("tm", None, "space", None), P("tm", None, "space", None)),
        check_vma=False,
    )
```
